32 devices in a mesh: groups: 2 (over x), ctx: 16 (over z, y, core).
Axes of the slice: x: 2, y: 2, z: 4, core: 2. Of those that a mesh axis runs over, the one named last changes fastest.
Arguments:
- hidden: bfloat16 [256, 8192], P('groups', 'ctx'), parts along dimension 0, may hold values from -6 to 6
- attn_gain: bfloat16 [8192], P('ctx'), may hold values from 0.25 to 1.75
- q_weight: bfloat16 [8192, 8192], P(None, 'ctx'), may hold values from -0.0625 to 0.0625
- q_gain: bfloat16 [128], replicated, may hold values from 0.25 to 1.75
- key_cache: bfloat16 [49152, 1024], P(('groups', 'ctx')), parts along dimension 0, may hold values from -64 to 64
- value_cache: bfloat16 [49152, 1024], P(('groups', 'ctx')), parts along dimension 0, may hold values from -6 to 6
- block_limit: int32 [256], P('groups'), parts along dimension 0, may hold values from 0 to 191, as said below
- out_weight: bfloat16 [8192, 8192], P('ctx'), may hold values from -0.09375 to 0.09375
- next_gain: bfloat16 [8192], P('ctx'), may hold values from 0.25 to 1.75
- next_weight: bfloat16 [8192, 8192], P(None, 'ctx'), may hold values from -0.0625 to 0.0625
Outputs:
- new_hidden: bfloat16 [256, 8192], P('groups', 'ctx'), parts along dimension 0
- next_queries: bfloat16 [256, 8192], P('groups', 'ctx'), parts along dimension 0
The draws below stay inside these ranges and needn't reach their ends.
There are 2 independent parts, one for each index of `groups`. The reference program is written for one: setup_inputs(seed, part) draws one part's arguments, and reference() takes and returns one part's arrays. A program takes and returns all parts, laid end to end along the dimension named above; an argument that names none is the same for every part. Nothing has to cross between parts.
Inputs may be any that keep to these rules, and one draw needn't show every extreme that they name: Text token i may attend the visual blocks 0 to block_limit[i], each of 128 visual tokens; some token reaches the last block and some only the first.
All inputs are finite; a program needn't handle non-finite values.
Results may differ from the reference program's by a relative error of at most 0.015.
Values may be sent and summed in bfloat16 or wider, within the bound.
A program may use at most 64 MiB of HBM per device.

```python
import jax
import jax.numpy as jnp
from jax import lax

D = 8192
HEADS = 64
KV_HEADS = 8
HEAD_DIM = 128
QUERIES = 128
BLK = 128
V_TOTAL = 24576
BLOCKS = 192


def draw_key_cache(key, part):
    first_key = jax.random.fold_in(jax.random.fold_in(key, 11), 0)
    shape = (V_TOTAL, KV_HEADS * HEAD_DIM)
    base = 3.0 * jax.random.truncated_normal(first_key, -6.0, 6.0, shape, jnp.float32)
    return base.astype(jnp.bfloat16)


def draw_block_limit(key, part):
    first_key, second_key, third_key = jax.random.split(jax.random.fold_in(key, 23), 3)
    limits = jax.random.randint(first_key, (QUERIES,), 0, BLOCKS)
    highest = jax.random.randint(second_key, (), 0, QUERIES)
    lowest = (highest + 1 + jax.random.randint(third_key, (), 0, QUERIES - 1)) % QUERIES
    limits = limits.at[highest].set(BLOCKS - 1).at[lowest].set(0)
    return limits.astype(jnp.int32)


def spiked(array, rng, source, target, shards_of, factor):
    def block_of(axis_at):
        return (jnp.arange(array.shape[axis_at]) // (array.shape[axis_at] // shards_of)).reshape((-1,) + (1,) * (array.ndim - 1 - axis_at))

    one_side = jax.random.permutation(rng, shards_of)[block_of(target)]
    far = (block_of(target) + shards_of // 2) % shards_of
    return jnp.where((block_of(source) == one_side) | (block_of(source) == far), factor * array, array)


def levels(key, extent, shards, low, top_value):
    loudness = 1.0
    for dim, blocks in shards:
        steps = jax.random.uniform(jax.random.fold_in(jax.random.fold_in(key, 6), dim), (blocks,), jnp.float32, low / len(shards), top_value / len(shards))
        loudness = loudness * jnp.repeat(jnp.exp(steps), extent[dim] // blocks).reshape((-1,) + (1,) * (len(extent) - 1 - dim))
    return loudness


def noise(stream_key, dims, scale, most, cuts=(), kind=jnp.bfloat16):
    values = jax.random.normal(stream_key, dims, jnp.float32) * scale
    if len(cuts) > 0:
        values = levels(stream_key, dims, cuts, -0.22, 0.18) * values
    return jnp.clip(values, min=-most, max=most).astype(kind)


def gaussian_with(key, extent, width, bound, pieces, heavy, held_as=jnp.bfloat16):
    entries = width * jax.random.normal(key, extent, jnp.float32)
    if pieces:
        entries = entries * levels(key, extent, pieces, -0.22, 0.18)
    return jnp.clip(spiked(entries, jax.random.fold_in(key, 3), *heavy), -bound, bound).astype(held_as)


def setup_inputs(seed: int = 0, part: int = 0) -> dict:
    seeds = jax.random.split(jax.random.key(seed), 11)
    part_splits = jax.random.split(jax.random.fold_in(seeds[10], part), 11)
    hidden = noise(part_splits[0], (QUERIES, D), 1.0, 6.0, ((1, 16),))
    attn_gain = jnp.clip(1.0 + 0.15 * jax.random.normal(seeds[1], (D,), jnp.float32), 0.25, 1.75).astype(jnp.bfloat16)
    q_weight = noise(seeds[2], (D, HEADS * HEAD_DIM), D ** -0.5, 0.0625, ((1, 16),))
    q_gain = jnp.clip(1.0 + 0.15 * jax.random.normal(seeds[3], (HEAD_DIM,), jnp.float32), 0.25, 1.75).astype(jnp.bfloat16)
    key_cache = draw_key_cache(jax.random.fold_in(jax.random.fold_in(seeds[10], part), 71), part)
    value_cache = noise(part_splits[5], (V_TOTAL, KV_HEADS * HEAD_DIM), 1.0, 6.0, ((0, 16),))
    block_limit = draw_block_limit(jax.random.fold_in(jax.random.fold_in(seeds[10], part), 71), part)
    out_weight = gaussian_with(seeds[7], (HEADS * HEAD_DIM, D), (HEADS * HEAD_DIM) ** -0.5, 0.09375, ((0, 16),), (0, 1, 16, 2.0))
    next_gain = jnp.clip(1.0 + 0.15 * jax.random.normal(seeds[8], (D,), jnp.float32), 0.25, 1.75).astype(jnp.bfloat16)
    next_weight = noise(seeds[9], (D, HEADS * HEAD_DIM), D ** -0.5, 0.0625, ((1, 16),))
    return {"hidden": hidden, "attn_gain": attn_gain, "q_weight": q_weight, "q_gain": q_gain, "key_cache": key_cache, "value_cache": value_cache, "block_limit": block_limit, "out_weight": out_weight, "next_gain": next_gain, "next_weight": next_weight}


def rms_rows(rows_in, gain):
    values = rows_in.astype(jnp.float32)
    square_mean = lax.optimization_barrier(jnp.mean(values * values, axis=-1, keepdims=True))
    return (values * lax.rsqrt(square_mean + 1e-05) * gain.astype(jnp.float32)).astype(jnp.bfloat16)

def reference(hidden, attn_gain, q_weight, q_gain, key_cache, value_cache, block_limit, out_weight, next_gain, next_weight):
    normed = rms_rows(hidden, attn_gain)
    query = jnp.dot(normed, q_weight, preferred_element_type=jnp.float32)
    query = query.reshape(QUERIES, HEADS, HEAD_DIM)
    head_mean = lax.optimization_barrier(jnp.mean(query * query, axis=-1, keepdims=True))
    query_normed = (query * lax.rsqrt(head_mean + 1e-05) * q_gain.astype(jnp.float32)).astype(jnp.bfloat16)
    positions = jnp.arange(V_TOTAL, dtype=jnp.int32) // BLK
    allowed = positions[None, :] <= block_limit[:, None]
    scale = HEAD_DIM ** (-0.5)
    per_group = HEADS // KV_HEADS

    def one_head(head):
        group = (head // per_group).astype(jnp.int32)
        keys = lax.dynamic_slice_in_dim(key_cache, group * HEAD_DIM, HEAD_DIM, 1)
        values = lax.dynamic_slice_in_dim(value_cache, group * HEAD_DIM, HEAD_DIM, 1)
        single = lax.dynamic_index_in_dim(query_normed, head, 1, keepdims=False)
        scores = jnp.dot(single, keys.T, preferred_element_type=jnp.float32) * scale
        scores = jnp.where(allowed, scores, -jnp.inf)
        top = lax.optimization_barrier(jnp.max(scores, axis=-1, keepdims=True))
        expo = jnp.exp(scores - top)
        denominator = lax.optimization_barrier(jnp.sum(expo, axis=-1, keepdims=True))
        summed = jnp.dot(expo.astype(jnp.bfloat16), values, preferred_element_type=jnp.float32)
        return (summed / denominator).astype(jnp.bfloat16)
    attended = lax.map(one_head, jnp.arange(HEADS, dtype=jnp.int32))
    attended = jnp.transpose(attended, (1, 0, 2)).reshape(QUERIES, HEADS * HEAD_DIM)
    mixed = jnp.dot(attended, out_weight, preferred_element_type=jnp.float32)
    new_hidden = (hidden.astype(jnp.float32) + mixed).astype(jnp.bfloat16)
    renormed = rms_rows(new_hidden, next_gain)
    next_queries = jnp.dot(renormed, next_weight, preferred_element_type=jnp.float32).astype(jnp.bfloat16)
    return (new_hidden, next_queries)
```

```python
import functools
import math

import jax
import jax.numpy as jnp
from jax import lax
from jax.experimental import pallas as pl
from jax.experimental.pallas import tpu as pltpu
from jax.sharding import PartitionSpec as P

BLK = 128
EPSILON = 1e-05
MESH = pl.DeviceIdType.MESH
BF16, F32 = jnp.bfloat16, jnp.float32


def loop(count, body):
    def step(i, carry):
        body(i)
        return carry

    lax.fori_loop(0, count, step, 0)


def kernel(
    n,
    group_size,
    pieces,
    hidden_in,
    attn_gain_ref,
    next_gain_ref,
    q_gain_ref,
    limit_ref,
    qw_hbm,
    key_hbm,
    value_hbm,
    ow_hbm,
    nw_hbm,
    hidden_out,
    next_out,
    qw,
    keys,
    values,
    ow,
    nw,
    first,
    first_squares,
    queries_all,
    second,
    second_squares,
    sums,
    stats,
    mixed,
    sums_core,
    stats_core,
    mixed_core,
    sums_y,
    stats_y,
    mixed_y,
    sums_up,
    stats_up,
    mixed_up,
    sums_down,
    stats_down,
    mixed_down,
    acc,
    squares,
    limits,
    attended,
    sems,
    local_sems,
):
    depth = n // 4
    me = lax.axis_index("ctx")
    core, y, z = lax.rem(me, 2), lax.rem(me // 2, 2), me // 4
    rows, width = hidden_out.shape
    features = n * width
    head_dim = q_gain_ref.shape[1]
    heads = width // head_dim
    tokens = keys.shape[0]

    def at(zz, yy, cc):
        return zz * 4 + yy * 2 + cc

    other_core, other_y = at(z, y, 1 - core), at(z, 1 - y, core)
    above, below = at(z + 1, y, core), at(z - 1, y, core)

    loads = [
        pltpu.make_async_copy(src, dst, local_sems.at[i])
        for i, (src, dst) in enumerate(
            [(qw_hbm, qw), (key_hbm, keys), (value_hbm, values), (ow_hbm, ow), (nw_hbm, nw)]
        )
    ]
    for load in loads:
        load.start()

    barrier = pltpu.get_barrier_semaphore()

    def greet(device):
        pl.semaphore_signal(barrier, inc=1, device_id={"ctx": device}, device_id_type=MESH)

    greet(other_core)
    greet(other_y)
    pl.when(z + 1 < depth)(lambda: greet(above))
    pl.when(z > 0)(lambda: greet(below))

    def lay_row(column):
        return jnp.broadcast_to(column, (rows, rows)).T[:1, :]

    def lay_column(row):
        return jnp.broadcast_to(row, (rows, rows)).T[:, :1]

    def lane_sums(part):
        squared = part * part
        total = squared[:, :BLK]
        for start in range(BLK, width, BLK):
            total += squared[:, start : start + BLK]
        return total

    own = hidden_in[...].astype(F32)
    first[me] = (own * attn_gain_ref[...].astype(F32)).astype(BF16)
    first_squares[me] = lay_row(jnp.sum(lane_sums(own), axis=1, keepdims=True))

    peers = 2 + jnp.where(z + 1 < depth, 1, 0) + jnp.where(z > 0, 1, 0)
    pl.semaphore_wait(barrier, peers)

    before, after = z, depth - 1 - z
    lone, paired = jnp.abs(after - before), jnp.minimum(after, before)

    def farthest(i):
        j = jnp.maximum(i - lone, 0)
        distance = paired - lax.div(j, 2)
        near = z + jnp.where(lax.rem(j, 2) == 0, distance, -distance)
        return jnp.where(i < lone, jnp.where(after > before, depth - 1 - i, i), near)

    def remote(src, dst, send, recv, device):
        return pltpu.make_async_remote_copy(
            src_ref=src,
            dst_ref=dst,
            send_sem=sems.at[send],
            recv_sem=sems.at[recv],
            device_id={"ctx": device},
            device_id_type=MESH,
        )

    used = [0]
    drains = []

    def take(count):
        used[0] += count
        return used[0] - count

    class Gather:
        def __init__(self, buffer, count, extra=None):
            self.buffer, self.count, self.extra = buffer, count, extra
            self.size = buffer.shape[1] // count
            self.recv, self.send = take(n * count), take(5 * depth)
            if extra is not None:
                self.extra_recv, self.extra_send = take(n), take(5 * depth)
            drains.append(self.drain)

        def copy(self, block, p, device, sem):
            view = self.buffer.at[block, pl.ds(pl.multiple_of(p * self.size, self.size), self.size)]
            return remote(view, view, self.send + sem, self.recv + block * self.count + p, device)

        def extra_copy(self, block, device, sem):
            view = self.extra.at[block]
            return remote(view, view, self.extra_send + sem, self.extra_recv + block, device)

        def whole(self, block, device, sem):
            view = self.buffer.at[block]
            return remote(view, view, self.send + sem, self.recv, device)

        def routes(self, zz):
            return (
                (at(zz, y, core), above, zz),
                (at(zz, y, core), below, depth + zz),
                (at(zz, y, core), other_y, 2 * depth + zz),
            )

        def to_core(self, zz, yy):
            return at(zz, yy, core), other_core, 3 * depth + 2 * zz + yy

        def start(self, route, p):
            block, device, sem = route
            if p is None:
                self.extra_copy(block, device, sem).start()
            else:
                self.copy(block, p, device, sem).start()

        def arrive(self, block, p):
            if p is None:
                self.extra_copy(block, other_core, 0).wait_recv()
            else:
                self.copy(block, p, other_core, 0).wait_recv()

        def arrive_all(self, block):
            loop(self.count, lambda p: self.arrive(block, p))
            if self.extra is not None:
                self.arrive(block, None)

        def begin(self, p):
            up, down, side = self.routes(z)
            pl.when(z + 1 < depth)(lambda: self.start(up, p))
            pl.when(z > 0)(lambda: self.start(down, p))
            self.start(side, p)
            self.start(self.to_core(z, y), p)

        def column(self, distance, sign, p):
            zz = z + sign * distance

            @pl.when((zz >= 0) & (zz < depth))
            def _():
                up, down, side = self.routes(zz)
                self.arrive(at(zz, y, core), p)
                if sign < 0:
                    pl.when(z + 1 < depth)(lambda: self.start(up, p))
                else:
                    pl.when(z > 0)(lambda: self.start(down, p))
                self.start(side, p)
                self.start(self.to_core(zz, y), p)

        def beside(self, distance, sign, p):
            zz = z + sign * distance
            fresh = (distance > 0) if sign > 0 else (distance >= 0)

            @pl.when((zz >= 0) & (zz < depth) & fresh)
            def _():
                self.arrive(at(zz, 1 - y, core), p)
                self.start(self.to_core(zz, 1 - y), p)

        def run(self, ready, consume, consume_late=None):
            def pair(distance, yy, cc, use):
                def one(i):
                    zz = z + jnp.where(i == 0, -distance, distance)
                    fresh = (distance > 0) | ((distance == 0) & (i == 0))

                    @pl.when(fresh & (zz >= 0) & (zz < depth))
                    def _():
                        use(at(zz, yy, cc))

                loop(2, one)

            def late(block):
                self.arrive_all(block)
                consume_late(block)

            def relay(step, p):
                self.column(step, -1, p)
                self.column(step, 1, p)
                self.beside(step - 1, -1, p)
                self.beside(step - 1, 1, p)

            def turn(i):
                step = i + 1

                def inner(p):
                    pl.when(step <= depth)(lambda: relay(step, p))
                    pl.when((step == 1) & (p == 0))(ready)
                    for k in range(4):
                        slot = (k * self.count) // 4

                        @pl.when(p == slot)
                        def _():
                            if k == 0:
                                pair(step - 1, y, core, consume)
                            elif k == 1:
                                pair(step - 2, 1 - y, core, consume)
                            elif consume_late is not None and k == 2:
                                pair(step - 2, y, 1 - core, late)
                            elif consume_late is not None:
                                pair(step - 3, 1 - y, 1 - core, late)

                loop(self.count, inner)
                if self.extra is not None:
                    pl.when(step <= depth)(lambda: relay(step, None))

            loop(depth + 2 if consume_late is not None else depth + 1, turn)

        def drain(self):
            kinds = [self.whole]
            if self.extra is not None:
                kinds.append(self.extra_copy)

            def one(zz):
                up, down, side = self.routes(zz)
                for kind in kinds:
                    pl.when((zz <= z) & (z + 1 < depth))(lambda: kind(*up).wait_send())
                    pl.when((zz >= z) & (z > 0))(lambda: kind(*down).wait_send())
                    kind(*side).wait_send()
                    kind(*self.to_core(zz, 0)).wait_send()
                    kind(*self.to_core(zz, 1)).wait_send()

            loop(depth, one)

    def reduce(arrays, count, compute_other, compute, combine, finish):
        starts = [(take(5 * depth), take(5 * depth * count)) for _ in arrays]

        def copies(kind, p, zz, yy=0):
            made = []
            for (send, recv), (view, part, from_core, from_y, from_below, from_above) in zip(starts, arrays):
                if kind == 0:
                    slot, where = 2 * zz + yy, 0
                    block, dst, device = at(zz, yy, 1 - core), from_core, other_core
                elif kind == 1:
                    slot, where = zz, 2 * depth
                    block, dst, device = at(zz, 1 - y, core), from_y, other_y
                elif kind == 2:
                    slot, where = zz, 3 * depth
                    block, dst, device = at(zz, y, core), from_below, above
                else:
                    slot, where = zz, 4 * depth
                    block, dst, device = at(zz, y, core), from_above, below
                if p is None:
                    src, dst, arrival = part.at[block], dst.at[slot], 0
                else:
                    src, dst, arrival = view(part, block, p), view(dst, slot, p), (where + slot) * count + p
                made.append(remote(src, dst, send + where + slot, recv + arrival, device))
            return made

        def begin(*which):
            for copy in copies(*which):
                copy.start()

        def received(*which):
            for copy in copies(*which):
                copy.wait_recv()

        def sent(*which):
            for copy in copies(*which):
                copy.wait_send()

        def add(block, p, which, slot):
            combine(block, p, [array[0](array[which], slot, p) for array in arrays])

        def spread(zz):
            def across(i):
                yy = jnp.where(i == 0, 1 - y, y)
                compute_other(at(zz, yy, 1 - core))
                loop(count, lambda p: begin(0, p, zz, yy))

            def here(i):
                yy = jnp.where(i == 0, 1 - y, y)
                block = at(zz, yy, core)
                compute(block)

                def one(p):
                    received(0, p, zz, yy)
                    add(block, p, 2, 2 * zz + yy)
                    pl.when(i == 0)(lambda: begin(1, p, zz))

                loop(count, one)

            loop(2, across)
            loop(2, here)

        def along(zz):
            block = at(zz, y, core)

            def one(p):
                received(1, p, zz)
                add(block, p, 3, zz)

                @pl.when(zz > z)
                def _():
                    @pl.when(z > 0)
                    def _():
                        received(2, p, zz)
                        add(block, p, 4, zz)

                    begin(2, p, zz)

                @pl.when(zz < z)
                def _():
                    @pl.when(z + 1 < depth)
                    def _():
                        received(3, p, zz)
                        add(block, p, 5, zz)

                    begin(3, p, zz)

            loop(count, one)

        def step(i):
            pl.when(i < depth)(lambda: spread(farthest(i)))
            pl.when(i > 0)(lambda: along(farthest(i - 1)))

        loop(depth + 1, step)

        def last(p):
            @pl.when(z > 0)
            def _():
                received(2, p, z)
                add(me, p, 4, z)

            @pl.when(z + 1 < depth)
            def _():
                received(3, p, z)
                add(me, p, 5, z)

            finish(p)

        loop(count, last)

        def drain():
            def one(zz):
                sent(0, None, zz, 0)
                sent(0, None, zz, 1)
                sent(1, None, zz)
                pl.when(zz > z)(lambda: sent(2, None, zz))
                pl.when(zz < z)(lambda: sent(3, None, zz))

            loop(depth, one)

        drains.append(drain)

    def project(gathered, weight, load):
        acc[...] = jnp.zeros_like(acc)

        def term(block):
            depth_rows = pl.ds(pl.multiple_of(block * width, width), width)
            acc[...] += jnp.dot(
                gathered.buffer[block], weight[depth_rows, :], preferred_element_type=F32
            )

        gathered.run(load.wait, term, term)
        mean = lay_column(jnp.sum(gathered.extra[...], axis=0)) * (1.0 / features)
        return acc[...] * lax.rsqrt(mean + EPSILON)

    gather_first = Gather(first, pieces, first_squares)
    gather_queries = Gather(queries_all, heads)
    gather_second = Gather(second, pieces, second_squares)

    loop(pieces, gather_first.begin)
    gather_first.begin(None)
    limit_rows = lay_column(limit_ref[...])
    for head in range(heads):
        limits[head * rows : (head + 1) * rows, :] = jnp.broadcast_to(limit_rows, (rows, BLK))

    query = project(gather_first, qw, loads[0])
    for head in range(heads):
        one = query[:, head * head_dim : (head + 1) * head_dim]
        mean = jnp.mean(one * one, axis=1, keepdims=True)
        queries_all[me, head * rows : (head + 1) * rows, :] = (
            one * lax.rsqrt(mean + EPSILON) * q_gain_ref[...].astype(F32)
        ).astype(BF16)
        gather_queries.begin(head)

    factor = head_dim**-0.5 * math.log2(math.e)
    first_block = me * (tokens // BLK)
    chunk = min(2 * rows, heads * rows)

    def attend(block):
        group = (block * heads) // group_size
        columns = pl.ds(pl.multiple_of(group * head_dim, head_dim), head_dim)
        for start in range(0, heads * rows, chunk):
            query_rows = queries_all[block, start : start + chunk, :]
            scores = lax.dot_general(
                query_rows, keys[:, columns], (((1,), (1,)), ((), ())), preferred_element_type=F32
            )
            limit = limits[start : start + chunk, :]
            tiles = [
                jnp.where(
                    limit >= first_block + j, scores[:, j * BLK : (j + 1) * BLK] * factor, -jnp.inf
                )
                for j in range(tokens // BLK)
            ]
            top = functools.reduce(jnp.maximum, tiles)
            top = jnp.maximum(jnp.max(top, axis=1, keepdims=True), -1e30)
            tiles = [jnp.exp2(tile - top) for tile in tiles]
            total = jnp.sum(functools.reduce(jnp.add, tiles), axis=1, keepdims=True)
            weights = jnp.concatenate([tile.astype(BF16) for tile in tiles], axis=1)
            summed = jnp.dot(weights, values[:, columns], preferred_element_type=F32)
            sums[block, start : start + chunk, :] = summed.astype(BF16)
            for inner in range(0, chunk, rows):
                head = (start + inner) // rows
                stats[block, head, 0:1, :] = lay_row(top[inner : inner + rows, :])
                stats[block, head, 1:2, :] = lay_row(total[inner : inner + rows, :])

    def span(head):
        return pl.ds(pl.multiple_of(head * rows, rows), rows)

    def merge(block, head, arrived):
        more_sums, more_stats = arrived
        mine, theirs = stats[block, head], more_stats[...]
        top = jnp.maximum(mine[:1], theirs[:1])
        decay, decay_more = jnp.exp2(mine[:1] - top), jnp.exp2(theirs[:1] - top)
        stats[block, head, 0:1, :] = top
        stats[block, head, 1:2, :] = mine[1:2] * decay + theirs[1:2] * decay_more
        sums[block, span(head), :] = (
            sums[block, span(head), :].astype(F32) * lay_column(decay)
            + more_sums[...].astype(F32) * lay_column(decay_more)
        ).astype(BF16)

    def caches_ready():
        loads[1].wait()
        loads[2].wait()

    gather_queries.run(caches_ready, attend)

    def attend_late(block):
        gather_queries.arrive_all(block)
        attend(block)

    def close(head):
        total = lay_column(stats[me, head, 1:2, :])
        attended[:, pl.ds(pl.multiple_of(head * head_dim, head_dim), head_dim)] = (
            sums[me, span(head), :].astype(F32) / total
        ).astype(BF16)

    def head_view(ref, block, p):
        return ref.at[block, span(p)]

    def stat_view(ref, block, p):
        return ref.at[block, p]

    reduce(
        [
            (head_view, sums, sums_core, sums_y, sums_up, sums_down),
            (stat_view, stats, stats_core, stats_y, stats_up, stats_down),
        ],
        heads,
        attend_late,
        lambda block: None,
        merge,
        close,
    )
    loads[3].wait()

    piece = rows // pieces

    def piece_rows(p):
        return pl.ds(pl.multiple_of(p * piece, piece), piece)

    def row_view(ref, block, p):
        return ref.at[block, piece_rows(p)]

    def mix(block):
        columns = pl.ds(pl.multiple_of(block * width, width), width)
        mixed[block] = jnp.dot(
            attended[...], ow[:, columns], preferred_element_type=F32
        ).astype(BF16)

    def total_of(block, p, arrived):
        mixed[block, piece_rows(p), :] = (
            mixed[block, piece_rows(p), :].astype(F32) + arrived[0][...].astype(F32)
        ).astype(BF16)

    def renew(p):
        span_rows = piece_rows(p)
        fresh = (hidden_in[span_rows, :].astype(F32) + mixed[me, span_rows, :].astype(F32)).astype(BF16)
        hidden_out[span_rows, :] = fresh
        fresh = fresh.astype(F32)
        second[me, span_rows, :] = (fresh * next_gain_ref[...].astype(F32)).astype(BF16)
        squares[span_rows, :] = lane_sums(fresh)
        gather_second.begin(p)

    reduce(
        [(row_view, mixed, mixed_core, mixed_y, mixed_up, mixed_down)], pieces, mix, mix, total_of, renew
    )
    second_squares[me] = lay_row(jnp.sum(squares[...], axis=1, keepdims=True))
    gather_second.begin(None)
    next_out[...] = project(gather_second, nw, loads[4]).astype(BF16)
    for drain in drains:
        drain()


def on_device(
    hidden,
    attn_gain,
    q_weight,
    q_gain,
    key_cache,
    value_cache,
    block_limit,
    out_weight,
    next_gain,
    next_weight,
):
    n = lax.axis_size("ctx")
    depth = n // 4
    rows, width = hidden.shape
    head_dim = q_gain.shape[0]
    heads = width // head_dim
    group_size = heads * n // (key_cache.shape[1] // head_dim)
    tall, pieces = heads * rows, 4

    def slots(count):
        return [
            pltpu.VMEM((count, tall, head_dim), BF16),
            pltpu.VMEM((count, heads, 2, rows), F32),
            pltpu.VMEM((count, rows, width), BF16),
        ]

    semaphores = 2 * n * (pieces + 1) + n * heads + 25 * depth + 5 * depth * (2 * heads + pieces + 3)
    vmem, hbm = pl.BlockSpec(memory_space=pltpu.VMEM), pl.BlockSpec(memory_space=pl.ANY)
    return pl.pallas_call(
        functools.partial(kernel, n, group_size, pieces),
        out_shape=[jax.ShapeDtypeStruct((rows, width), BF16)] * 2,
        in_specs=[vmem] * 5 + [hbm] * 5,
        out_specs=[vmem] * 2,
        scratch_shapes=[
            pltpu.VMEM(q_weight.shape, BF16),
            pltpu.VMEM(key_cache.shape, BF16),
            pltpu.VMEM(value_cache.shape, BF16),
            pltpu.VMEM(out_weight.shape, BF16),
            pltpu.VMEM(next_weight.shape, BF16),
            pltpu.VMEM((n, rows, width), BF16),
            pltpu.VMEM((n, 1, rows), F32),
            pltpu.VMEM((n, tall, head_dim), BF16),
            pltpu.VMEM((n, rows, width), BF16),
            pltpu.VMEM((n, 1, rows), F32),
            *slots(n),
            *slots(2 * depth),
            *slots(depth),
            *slots(depth),
            *slots(depth),
            pltpu.VMEM((rows, width), F32),
            pltpu.VMEM((rows, BLK), F32),
            pltpu.VMEM((tall, BLK), jnp.int32),
            pltpu.VMEM((rows, width), BF16),
            pltpu.SemaphoreType.DMA((semaphores,)),
            pltpu.SemaphoreType.DMA((5,)),
        ],
        compiler_params=pltpu.CompilerParams(
            collective_id=0, has_side_effects=True, vmem_limit_bytes=67043328
        ),
    )(
        hidden,
        attn_gain[None],
        next_gain[None],
        q_gain[None],
        block_limit[None],
        q_weight,
        key_cache,
        value_cache,
        out_weight,
        next_weight,
    )


def solution(mesh):
    in_specs = (
        P("groups", "ctx"),
        P("ctx"),
        P(None, "ctx"),
        P(),
        P(("groups", "ctx"), None),
        P(("groups", "ctx"), None),
        P("groups"),
        P("ctx", None),
        P("ctx"),
        P(None, "ctx"),
    )
    out_specs = (P("groups", "ctx"), P("groups", "ctx"))

    def step(*args):
        return tuple(on_device(*args))

    return jax.shard_map(step, mesh=mesh, in_specs=in_specs, out_specs=out_specs, check_vma=False)
```

```python
import functools
import math

import jax
import jax.numpy as jnp
from jax import lax
from jax.experimental import pallas as pl
from jax.experimental.pallas import tpu as pltpu
from jax.sharding import PartitionSpec as P

BLK = 128
EPSILON = 1e-05
MESH = pl.DeviceIdType.MESH
BF16, F32 = jnp.bfloat16, jnp.float32


def loop(count, body):
    def step(i, carry):
        body(i)
        return carry

    lax.fori_loop(0, count, step, 0)


def kernel(
    n,
    group_size,
    pieces,
    hidden_in,
    attn_gain_ref,
    next_gain_ref,
    q_gain_ref,
    limit_ref,
    qw_hbm,
    key_hbm,
    value_hbm,
    ow_hbm,
    nw_hbm,
    hidden_out,
    next_out,
    qw,
    keys,
    values,
    ow,
    nw,
    first,
    first_squares,
    queries_all,
    second,
    second_squares,
    sums,
    stats,
    mixed,
    sums_core,
    stats_core,
    mixed_core,
    sums_y,
    stats_y,
    mixed_y,
    sums_z,
    stats_z,
    mixed_z,
    acc,
    squares,
    bias,
    marks,
    attended,
    sems,
    local_sems,
):
    depth = n // 4
    me = lax.axis_index("ctx")
    core, y, z = lax.rem(me, 2), lax.rem(me // 2, 2), me // 4
    rows, width = hidden_out.shape
    features = n * width
    head_dim = q_gain_ref.shape[1]
    heads = width // head_dim
    tokens = keys.shape[0]

    def at(zz, yy, cc):
        return zz * 4 + yy * 2 + cc

    other_core, other_y = at(z, y, 1 - core), at(z, 1 - y, core)

    def others(action):
        def one(zz):
            pl.when(zz != z)(lambda: action(zz))

        loop(depth, one)

    loads = [
        pltpu.make_async_copy(src, dst, local_sems.at[i])
        for i, (src, dst) in enumerate(
            [(qw_hbm, qw), (key_hbm, keys), (value_hbm, values), (ow_hbm, ow), (nw_hbm, nw)]
        )
    ]
    for load in loads:
        load.start()

    barrier = pltpu.get_barrier_semaphore()

    def greet(device):
        pl.semaphore_signal(barrier, inc=1, device_id={"ctx": device}, device_id_type=MESH)

    greet(other_core)
    greet(other_y)
    others(lambda zz: greet(at(zz, y, core)))

    def wide(gain):
        lines = gain[...].astype(F32)
        return jnp.concatenate([lines[i : i + 1, :] for i in range(lines.shape[0])], axis=1)

    def lay_row(column):
        return jnp.broadcast_to(column, (rows, rows)).T[:1, :]

    def lay_column(row):
        return jnp.broadcast_to(row, (rows, rows)).T[:, :1]

    def lane_sums(part):
        squared = part * part
        total = squared[:, :BLK]
        for start in range(BLK, width, BLK):
            total += squared[:, start : start + BLK]
        return total

    own = hidden_in[...].astype(F32)
    first[me] = (own * wide(attn_gain_ref)).astype(BF16)
    first_squares[me] = lay_row(jnp.sum(lane_sums(own), axis=1, keepdims=True))

    pl.semaphore_wait(barrier, depth + 1)

    before, after = z, depth - 1 - z
    lone, paired = jnp.abs(after - before), jnp.minimum(after, before)

    def farthest(i):
        j = jnp.maximum(i - lone, 0)
        distance = paired - lax.div(j, 2)
        near = z + jnp.where(lax.rem(j, 2) == 0, distance, -distance)
        return jnp.where(i < lone, jnp.where(after > before, depth - 1 - i, i), near)

    def remote(src, dst, send, recv, device):
        return pltpu.make_async_remote_copy(
            src_ref=src,
            dst_ref=dst,
            send_sem=sems.at[send],
            recv_sem=sems.at[recv],
            device_id={"ctx": device},
            device_id_type=MESH,
        )

    used = [0]
    drains = []

    def take(count):
        used[0] += count
        return used[0] - count

    class Gather:
        def __init__(self, buffer, count, extra=None):
            self.buffer, self.count, self.extra = buffer, count, extra
            self.size = buffer.shape[1] // count
            self.recv, self.send = take(n * count), take(4 * depth)
            if extra is not None:
                self.extra_recv, self.extra_send = take(n), take(4 * depth)
            drains.append(self.drain)

        def copy(self, block, p, device, sem):
            view = self.buffer.at[block, pl.ds(pl.multiple_of(p * self.size, self.size), self.size)]
            return remote(view, view, self.send + sem, self.recv + block * self.count + p, device)

        def extra_copy(self, block, device, sem):
            view = self.extra.at[block]
            return remote(view, view, self.extra_send + sem, self.extra_recv + block, device)

        def whole(self, block, device, sem):
            view = self.buffer.at[block]
            return remote(view, view, self.send + sem, self.recv, device)

        def to_z(self, zz):
            return me, at(zz, y, core), zz

        def to_y(self, zz):
            return at(zz, y, core), other_y, depth + zz

        def to_core(self, zz, yy):
            return at(zz, yy, core), other_core, 2 * depth + 2 * zz + yy

        def start(self, route, p):
            block, device, sem = route
            if p is None:
                self.extra_copy(block, device, sem).start()
            else:
                self.copy(block, p, device, sem).start()

        def arrive(self, block, p):
            if p is None:
                self.extra_copy(block, other_core, 0).wait_recv()
            else:
                self.copy(block, p, other_core, 0).wait_recv()

        def arrive_all(self, block):
            loop(self.count, lambda p: self.arrive(block, p))
            if self.extra is not None:
                self.arrive(block, None)

        def begin(self, p):
            self.start(self.to_y(z), p)
            others(lambda zz: self.start(self.to_z(zz), p))
            self.start(self.to_core(z, y), p)

        def column(self, distance, sign, p):
            zz = z + sign * distance

            @pl.when((zz >= 0) & (zz < depth))
            def _():
                self.arrive(at(zz, y, core), p)
                self.start(self.to_y(zz), p)
                self.start(self.to_core(zz, y), p)

        def beside(self, distance, sign, p):
            zz = z + sign * distance
            fresh = (distance > 0) if sign > 0 else (distance >= 0)

            @pl.when((zz >= 0) & (zz < depth) & fresh)
            def _():
                self.arrive(at(zz, 1 - y, core), p)
                self.start(self.to_core(zz, 1 - y), p)

        def run(self, ready, consume, consume_late=None):
            def pair(distance, yy, cc, use):
                def one(i):
                    zz = z + jnp.where(i == 0, -distance, distance)
                    fresh = (distance > 0) | ((distance == 0) & (i == 0))

                    @pl.when(fresh & (zz >= 0) & (zz < depth))
                    def _():
                        use(at(zz, yy, cc))

                loop(2, one)

            def late(block):
                self.arrive_all(block)
                consume_late(block)

            def relay(step, p):
                self.column(step, -1, p)
                self.column(step, 1, p)
                self.beside(step - 1, -1, p)
                self.beside(step - 1, 1, p)

            def turn(i):
                step = i + 1

                def inner(p):
                    pl.when(step <= depth)(lambda: relay(step, p))
                    pl.when((step == 1) & (p == 0))(ready)
                    for k in range(4):
                        slot = (k * self.count) // 4

                        @pl.when(p == slot)
                        def _():
                            if k == 0:
                                pair(step - 1, y, core, consume)
                            elif k == 1:
                                pair(step - 2, 1 - y, core, consume)
                            elif consume_late is not None and k == 2:
                                pair(step - 2, y, 1 - core, late)
                            elif consume_late is not None:
                                pair(step - 3, 1 - y, 1 - core, late)

                loop(self.count, inner)
                if self.extra is not None:
                    pl.when(step <= depth)(lambda: relay(step, None))

            loop(depth + 2 if consume_late is not None else depth + 1, turn)

        def drain(self):
            kinds = [self.whole]
            if self.extra is not None:
                kinds.append(self.extra_copy)

            def one(zz):
                for kind in kinds:
                    pl.when(zz != z)(lambda: kind(*self.to_z(zz)).wait_send())
                    kind(*self.to_y(zz)).wait_send()
                    kind(*self.to_core(zz, 0)).wait_send()
                    kind(*self.to_core(zz, 1)).wait_send()

            loop(depth, one)

    def reduce(arrays, count, compute_other, compute, combine, finish):
        starts = [(take(4 * depth), take(4 * depth * count)) for _ in arrays]

        def copies(kind, p, zz, yy=0):
            made = []
            for (send, recv), (view, part, from_core, from_y, from_z) in zip(starts, arrays):
                sender = slot = zz
                if kind == 0:
                    sender = slot = 2 * zz + yy
                    where, block, dst, device = 0, at(zz, yy, 1 - core), from_core, other_core
                elif kind == 1:
                    where, block, dst, device = 2 * depth, at(zz, 1 - y, core), from_y, other_y
                else:
                    where, block, dst, device = 3 * depth, at(zz, y, core), from_z, at(zz, y, core)
                    slot = z if kind == 2 else zz
                if p is None:
                    src, dst, arrival = part.at[block], dst.at[slot], 0
                else:
                    src, dst, arrival = view(part, block, p), view(dst, slot, p), (where + slot) * count + p
                made.append(remote(src, dst, send + where + sender, recv + arrival, device))
            return made

        def begin(*which):
            for copy in copies(*which):
                copy.start()

        def received(*which):
            for copy in copies(*which):
                copy.wait_recv()

        def sent(*which):
            for copy in copies(*which):
                copy.wait_send()

        def add(block, p, which, slot):
            combine(block, p, [array[0](array[which], slot, p) for array in arrays])

        def spread(zz):
            def across(i):
                yy = jnp.where(i == 0, 1 - y, y)
                compute_other(at(zz, yy, 1 - core))
                loop(count, lambda p: begin(0, p, zz, yy))

            def here(i):
                yy = jnp.where(i == 0, 1 - y, y)
                block = at(zz, yy, core)
                compute(block)

                def one(p):
                    received(0, p, zz, yy)
                    add(block, p, 2, 2 * zz + yy)
                    pl.when(i == 0)(lambda: begin(1, p, zz))

                loop(count, one)

            loop(2, across)
            loop(2, here)

        def along(zz):
            block = at(zz, y, core)

            def one(p):
                received(1, p, zz)
                add(block, p, 3, zz)
                pl.when(zz != z)(lambda: begin(2, p, zz))

            loop(count, one)

        def step(i):
            pl.when(i < depth)(lambda: spread(farthest(i)))
            pl.when(i > 0)(lambda: along(farthest(i - 1)))

        loop(depth + 1, step)

        def last(p):
            def one(zz):
                received(3, p, zz)
                add(me, p, 4, zz)

            others(one)
            finish(p)

        loop(count, last)

        def drain():
            def one(zz):
                sent(0, None, zz, 0)
                sent(0, None, zz, 1)
                sent(1, None, zz)
                pl.when(zz != z)(lambda: sent(2, None, zz))

            loop(depth, one)

        drains.append(drain)

    def project(gathered, weight, load):
        acc[...] = jnp.zeros_like(acc)

        def term(block):
            depth_rows = pl.ds(pl.multiple_of(block * width, width), width)
            acc[...] += jnp.dot(
                gathered.buffer[block], weight[depth_rows, :], preferred_element_type=F32
            )

        gathered.run(load.wait, term, term)
        mean = lay_column(jnp.sum(gathered.extra[...], axis=0)) * (1.0 / features)
        return acc[...] * lax.rsqrt(mean + EPSILON)

    gather_first = Gather(first, pieces, first_squares)
    gather_queries = Gather(queries_all, heads)
    gather_second = Gather(second, pieces, second_squares)

    loop(pieces, gather_first.begin)
    gather_first.begin(None)
    factor = head_dim**-0.5 * math.log2(math.e)
    first_block = me * (tokens // BLK)
    chunk = min(2 * rows, heads * rows)
    lanes = lax.broadcasted_iota(jnp.int32, (rows, BLK), 1)
    limit_rows = lay_column(limit_ref[...])
    for start in range(0, chunk, rows):
        bias[start : start + rows, :] = jnp.where(limit_rows >= first_block + lanes, 0.0, -1e30).astype(BF16)
    lanes = lax.broadcasted_iota(jnp.int32, (BLK, BLK), 1)
    for j in range(tokens // BLK):
        marks[j * BLK : (j + 1) * BLK, :] = jnp.where(lanes == j, 1.0, 0.0).astype(BF16)

    query = project(gather_first, qw, loads[0])
    for head in range(heads):
        one = query[:, head * head_dim : (head + 1) * head_dim]
        mean = jnp.mean(one * one, axis=1, keepdims=True)
        queries_all[me, head * rows : (head + 1) * rows, :] = (
            one * lax.rsqrt(mean + EPSILON) * (q_gain_ref[...].astype(F32) * factor)
        ).astype(BF16)
        gather_queries.begin(head)

    def attend(block):
        group = (block * heads) // group_size
        columns = pl.ds(pl.multiple_of(group * head_dim, head_dim), head_dim)
        for start in range(0, heads * rows, chunk):
            query_rows = jnp.concatenate([queries_all[block, start : start + chunk, :], bias[...]], axis=1)
            marked = jnp.concatenate([keys[:, columns], marks[...]], axis=1)
            scores = lax.dot_general(
                query_rows, marked, (((1,), (1,)), ((), ())), preferred_element_type=F32
            )
            tiles = [scores[:, j * BLK : (j + 1) * BLK] for j in range(tokens // BLK)]
            top = functools.reduce(jnp.maximum, tiles)
            top = jnp.max(top, axis=1, keepdims=True)
            tiles = [jnp.exp2(tile - top) for tile in tiles]
            total = jnp.sum(functools.reduce(jnp.add, tiles), axis=1, keepdims=True)
            weights = jnp.concatenate([tile.astype(BF16) for tile in tiles], axis=1)
            summed = jnp.dot(weights, values[:, columns], preferred_element_type=F32)
            sums[block, start : start + chunk, :] = summed.astype(BF16)
            for inner in range(0, chunk, rows):
                head = (start + inner) // rows
                stats[block, head, 0:1, :] = lay_row(top[inner : inner + rows, :])
                stats[block, head, 1:2, :] = lay_row(total[inner : inner + rows, :])

    def span(head):
        return pl.ds(pl.multiple_of(head * rows, rows), rows)

    def merge(block, head, arrived):
        more_sums, more_stats = arrived
        mine, theirs = stats[block, head], more_stats[...]
        top = jnp.maximum(mine[:1], theirs[:1])
        decay, decay_more = jnp.exp2(mine[:1] - top), jnp.exp2(theirs[:1] - top)
        stats[block, head, 0:1, :] = top
        stats[block, head, 1:2, :] = mine[1:2] * decay + theirs[1:2] * decay_more
        sums[block, span(head), :] = (
            sums[block, span(head), :].astype(F32) * lay_column(decay)
            + more_sums[...].astype(F32) * lay_column(decay_more)
        ).astype(BF16)

    def caches_ready():
        loads[1].wait()
        loads[2].wait()

    gather_queries.run(caches_ready, attend)

    def attend_late(block):
        gather_queries.arrive_all(block)
        attend(block)

    def close(head):
        total = lay_column(stats[me, head, 1:2, :])
        attended[:, pl.ds(pl.multiple_of(head * head_dim, head_dim), head_dim)] = (
            sums[me, span(head), :].astype(F32) / total
        ).astype(BF16)

    def head_view(ref, block, p):
        return ref.at[block, span(p)]

    def stat_view(ref, block, p):
        return ref.at[block, p]

    reduce(
        [
            (head_view, sums, sums_core, sums_y, sums_z),
            (stat_view, stats, stats_core, stats_y, stats_z),
        ],
        heads,
        attend_late,
        lambda block: None,
        merge,
        close,
    )
    loads[3].wait()

    piece = rows // pieces

    def piece_rows(p):
        return pl.ds(pl.multiple_of(p * piece, piece), piece)

    def row_view(ref, block, p):
        return ref.at[block, piece_rows(p)]

    def mix(block):
        columns = pl.ds(pl.multiple_of(block * width, width), width)
        mixed[block] = jnp.dot(
            attended[...], ow[:, columns], preferred_element_type=F32
        ).astype(BF16)

    def total_of(block, p, arrived):
        mixed[block, piece_rows(p), :] = (
            mixed[block, piece_rows(p), :].astype(F32) + arrived[0][...].astype(F32)
        ).astype(BF16)

    def renew(p):
        span_rows = piece_rows(p)
        fresh = (hidden_in[span_rows, :].astype(F32) + mixed[me, span_rows, :].astype(F32)).astype(BF16)
        hidden_out[span_rows, :] = fresh
        fresh = fresh.astype(F32)
        second[me, span_rows, :] = (fresh * wide(next_gain_ref)).astype(BF16)
        squares[span_rows, :] = lane_sums(fresh)
        gather_second.begin(p)

    reduce(
        [(row_view, mixed, mixed_core, mixed_y, mixed_z)], pieces, mix, mix, total_of, renew
    )
    second_squares[me] = lay_row(jnp.sum(squares[...], axis=1, keepdims=True))
    gather_second.begin(None)
    next_out[...] = project(gather_second, nw, loads[4]).astype(BF16)
    for drain in drains:
        drain()


def on_device(
    hidden,
    attn_gain,
    q_weight,
    q_gain,
    key_cache,
    value_cache,
    block_limit,
    out_weight,
    next_gain,
    next_weight,
):
    n = lax.axis_size("ctx")
    depth = n // 4
    rows, width = hidden.shape
    head_dim = q_gain.shape[0]
    heads = width // head_dim
    group_size = heads * n // (key_cache.shape[1] // head_dim)
    tall, pieces = heads * rows, 4

    def slots(count):
        return [
            pltpu.VMEM((count, tall, head_dim), BF16),
            pltpu.VMEM((count, heads, 2, rows), F32),
            pltpu.VMEM((count, rows, width), BF16),
        ]

    semaphores = 2 * n * (pieces + 1) + n * heads + 20 * depth + 4 * depth * (2 * heads + pieces + 3)
    vmem, hbm = pl.BlockSpec(memory_space=pltpu.VMEM), pl.BlockSpec(memory_space=pl.ANY)
    outs = pl.pallas_call(
        functools.partial(kernel, n, group_size, pieces),
        out_shape=[jax.ShapeDtypeStruct((rows, width), BF16)] * 2,
        in_specs=[vmem] * 5 + [hbm] * 5,
        out_specs=[vmem] * 2,
        scratch_shapes=[
            pltpu.VMEM(q_weight.shape, BF16),
            pltpu.VMEM(key_cache.shape, BF16),
            pltpu.VMEM(value_cache.shape, BF16),
            pltpu.VMEM(out_weight.shape, BF16),
            pltpu.VMEM(next_weight.shape, BF16),
            pltpu.VMEM((n, rows, width), BF16),
            pltpu.VMEM((n, 1, rows), F32),
            pltpu.VMEM((n, tall, head_dim), BF16),
            pltpu.VMEM((n, rows, width), BF16),
            pltpu.VMEM((n, 1, rows), F32),
            *slots(n),
            *slots(2 * depth),
            *slots(depth),
            *slots(depth),
            pltpu.VMEM((rows, width), F32),
            pltpu.VMEM((rows, BLK), F32),
            pltpu.VMEM((min(2 * rows, tall), BLK), BF16),
            pltpu.VMEM((key_cache.shape[0], BLK), BF16),
            pltpu.VMEM((rows, width), BF16),
            pltpu.SemaphoreType.DMA((semaphores,)),
            pltpu.SemaphoreType.DMA((5,)),
        ],
        compiler_params=pltpu.CompilerParams(
            collective_id=0, has_side_effects=True, vmem_limit_bytes=67043328
        ),
    )(
        hidden,
        attn_gain.reshape(-1, BLK),
        next_gain.reshape(-1, BLK),
        q_gain[None],
        block_limit[None],
        q_weight,
        key_cache,
        value_cache,
        out_weight,
        next_weight,
    )
    return pl.pallas_call(
        hand_over,
        out_shape=[jax.ShapeDtypeStruct((rows, width), BF16)] * 2,
        in_specs=[vmem] * 2,
        out_specs=[vmem] * 2,
    )(*outs)


def hand_over(hidden_in, next_in, hidden_out, next_out):
    hidden_out[...] = hidden_in[...]
    next_out[...] = next_in[...]


def solution(mesh):
    in_specs = (
        P("groups", "ctx"),
        P("ctx"),
        P(None, "ctx"),
        P(),
        P(("groups", "ctx"), None),
        P(("groups", "ctx"), None),
        P("groups"),
        P("ctx", None),
        P("ctx"),
        P(None, "ctx"),
    )
    out_specs = (P("groups", "ctx"), P("groups", "ctx"))

    def step(*args):
        return tuple(on_device(*args))

    return jax.shard_map(step, mesh=mesh, in_specs=in_specs, out_specs=out_specs, check_vma=False)
```

```python
import functools
import math

import jax
import jax.numpy as jnp
from jax import lax
from jax.experimental import pallas as pl
from jax.experimental.pallas import tpu as pltpu
from jax.sharding import PartitionSpec as P

BLK = 128
EPSILON = 1e-05
MESH = pl.DeviceIdType.MESH
BF16, F32 = jnp.bfloat16, jnp.float32


def loop(count, body):
    def step(i, carry):
        body(i)
        return carry

    lax.fori_loop(0, count, step, 0)


def kernel(
    n,
    group_size,
    pieces,
    hidden_in,
    attn_gain_ref,
    next_gain_ref,
    q_gain_ref,
    limit_ref,
    qw_hbm,
    key_hbm,
    value_hbm,
    ow_hbm,
    nw_hbm,
    hidden_out,
    next_out,
    qw,
    keys,
    values,
    ow,
    nw,
    first,
    first_squares,
    queries_all,
    second,
    second_squares,
    sums,
    stats,
    mixed,
    sums_core,
    stats_core,
    mixed_core,
    sums_y,
    stats_y,
    mixed_y,
    sums_z,
    stats_z,
    mixed_z,
    acc,
    squares,
    bias,
    marks,
    attended,
    sems,
    local_sems,
):
    depth = n // 4
    me = lax.axis_index("ctx")
    core, y, z = lax.rem(me, 2), lax.rem(me // 2, 2), me // 4
    rows, width = hidden_out.shape
    features = n * width
    head_dim = q_gain_ref.shape[1]
    heads = width // head_dim
    tokens = keys.shape[0]

    def at(zz, yy, cc):
        return zz * 4 + yy * 2 + cc

    other_core, other_y = at(z, y, 1 - core), at(z, 1 - y, core)

    def others(action):
        def one(zz):
            pl.when(zz != z)(lambda: action(zz))

        loop(depth, one)

    loads = [
        pltpu.make_async_copy(src, dst, local_sems.at[i])
        for i, (src, dst) in enumerate(
            [(qw_hbm, qw), (key_hbm, keys), (value_hbm, values), (ow_hbm, ow), (nw_hbm, nw)]
        )
    ]
    for load in loads:
        load.start()

    barrier = pltpu.get_barrier_semaphore()

    def greet(device):
        pl.semaphore_signal(barrier, inc=1, device_id={"ctx": device}, device_id_type=MESH)

    greet(other_core)
    greet(other_y)
    others(lambda zz: greet(at(zz, y, core)))

    def wide(gain):
        lines = gain[...].astype(F32)
        return jnp.concatenate([lines[i : i + 1, :] for i in range(lines.shape[0])], axis=1)

    def lay_row(column):
        return jnp.broadcast_to(column, (rows, rows)).T[:1, :]

    def lay_column(row):
        return jnp.broadcast_to(row, (rows, rows)).T[:, :1]

    def lane_sums(part):
        squared = part * part
        total = squared[:, :BLK]
        for start in range(BLK, width, BLK):
            total += squared[:, start : start + BLK]
        return total

    own = hidden_in[...].astype(F32)
    first[me] = (own * wide(attn_gain_ref)).astype(BF16)
    first_squares[me] = lay_row(jnp.sum(lane_sums(own), axis=1, keepdims=True))

    pl.semaphore_wait(barrier, depth + 1)

    before, after = z, depth - 1 - z
    lone, paired = jnp.abs(after - before), jnp.minimum(after, before)

    def farthest(i):
        j = jnp.maximum(i - lone, 0)
        distance = paired - lax.div(j, 2)
        near = z + jnp.where(lax.rem(j, 2) == 0, distance, -distance)
        return jnp.where(i < lone, jnp.where(after > before, depth - 1 - i, i), near)

    def remote(src, dst, send, recv, device):
        return pltpu.make_async_remote_copy(
            src_ref=src,
            dst_ref=dst,
            send_sem=sems.at[send],
            recv_sem=sems.at[recv],
            device_id={"ctx": device},
            device_id_type=MESH,
        )

    used = [0]
    drains = []

    def take(count):
        used[0] += count
        return used[0] - count

    class Gather:
        def __init__(self, buffer, count, extra=None):
            self.buffer, self.count, self.extra = buffer, count, extra
            self.size = buffer.shape[1] // count
            self.recv, self.send = take(n * count), take(4 * depth)
            if extra is not None:
                self.extra_recv, self.extra_send = take(n), take(4 * depth)
            drains.append(self.drain)

        def copy(self, block, p, device, sem):
            view = self.buffer.at[block, pl.ds(pl.multiple_of(p * self.size, self.size), self.size)]
            return remote(view, view, self.send + sem, self.recv + block * self.count + p, device)

        def extra_copy(self, block, device, sem):
            view = self.extra.at[block]
            return remote(view, view, self.extra_send + sem, self.extra_recv + block, device)

        def whole(self, block, device, sem):
            view = self.buffer.at[block]
            return remote(view, view, self.send + sem, self.recv, device)

        def to_z(self, zz):
            return me, at(zz, y, core), zz

        def to_y(self, zz):
            return at(zz, y, core), other_y, depth + zz

        def to_core(self, zz, yy):
            return at(zz, yy, core), other_core, 2 * depth + 2 * zz + yy

        def start(self, route, p):
            block, device, sem = route
            if p is None:
                self.extra_copy(block, device, sem).start()
            else:
                self.copy(block, p, device, sem).start()

        def arrive(self, block, p):
            if p is None:
                self.extra_copy(block, other_core, 0).wait_recv()
            else:
                self.copy(block, p, other_core, 0).wait_recv()

        def arrive_all(self, block):
            loop(self.count, lambda p: self.arrive(block, p))
            if self.extra is not None:
                self.arrive(block, None)

        def begin(self, p):
            self.start(self.to_y(z), p)
            others(lambda zz: self.start(self.to_z(zz), p))
            self.start(self.to_core(z, y), p)

        def column(self, distance, sign, p):
            zz = z + sign * distance

            @pl.when((zz >= 0) & (zz < depth))
            def _():
                self.arrive(at(zz, y, core), p)
                self.start(self.to_y(zz), p)
                self.start(self.to_core(zz, y), p)

        def beside(self, distance, sign, p):
            zz = z + sign * distance
            fresh = (distance > 0) if sign > 0 else (distance >= 0)

            @pl.when((zz >= 0) & (zz < depth) & fresh)
            def _():
                self.arrive(at(zz, 1 - y, core), p)
                self.start(self.to_core(zz, 1 - y), p)

        def run(self, ready, consume, consume_late, reach):
            def pair(distance, yy, cc, use):
                def one(i):
                    zz = z + jnp.where(i == 0, -distance, distance)
                    fresh = (distance > 0) | ((distance == 0) & (i == 0))

                    @pl.when(fresh & (zz >= 0) & (zz < depth))
                    def _():
                        use(at(zz, yy, cc))

                loop(2, one)

            def late(block):
                self.arrive_all(block)
                consume_late(block)

            def relay(step, p):
                self.column(step, -1, p)
                self.column(step, 1, p)
                self.beside(step - 1, -1, p)
                self.beside(step - 1, 1, p)

            def turn(i):
                step = i + 1

                def inner(p):
                    pl.when(step <= depth)(lambda: relay(step, p))
                    pl.when((step == 1) & (p == 0))(ready)
                    for k in range(4):
                        slot = (k * self.count) // 4

                        @pl.when(p == slot)
                        def _():
                            if k == 0:
                                pair(step - 1, y, core, consume)
                            elif k == 1:
                                pair(step - 2, 1 - y, core, consume)
                            elif k == 2:
                                pl.when(step - 2 < reach)(lambda: pair(step - 2, y, 1 - core, late))
                            else:
                                pl.when(step - 3 < reach)(lambda: pair(step - 3, 1 - y, 1 - core, late))

                loop(self.count, inner)
                if self.extra is not None:
                    pl.when(step <= depth)(lambda: relay(step, None))

            loop(max(depth + 1, reach + 2), turn)

        def drain(self):
            kinds = [self.whole]
            if self.extra is not None:
                kinds.append(self.extra_copy)

            def one(zz):
                for kind in kinds:
                    pl.when(zz != z)(lambda: kind(*self.to_z(zz)).wait_send())
                    kind(*self.to_y(zz)).wait_send()
                    kind(*self.to_core(zz, 0)).wait_send()
                    kind(*self.to_core(zz, 1)).wait_send()

            loop(depth, one)

    def reduce(arrays, count, compute_other, compute, combine, finish):
        starts = [(take(4 * depth), take(2 * depth + 2 * depth * count)) for _ in arrays]

        def copies(kind, p, zz, yy=0):
            made = []
            for (send, recv), (view, part, from_core, from_y, from_z) in zip(starts, arrays):
                sender = slot = zz
                if kind == 0:
                    sender = slot = 2 * zz + yy
                    where, block, dst, device = 0, at(zz, yy, 1 - core), from_core, other_core
                elif kind == 1:
                    where, block, dst, device = 2 * depth, at(zz, 1 - y, core), from_y, other_y
                else:
                    where, block, dst, device = 3 * depth, at(zz, y, core), from_z, at(zz, y, core)
                    slot = z if kind == 2 else zz
                if p is None:
                    src, dst, arrival = part.at[block], dst.at[slot], slot if kind == 0 else 0
                else:
                    src, dst = view(part, block, p), view(dst, slot, p)
                    arrival = 2 * depth + (where - 2 * depth + slot) * count + p
                made.append(remote(src, dst, send + where + sender, recv + arrival, device))
            return made

        def begin(*which):
            for copy in copies(*which):
                copy.start()

        def received(*which):
            for copy in copies(*which):
                copy.wait_recv()

        def sent(*which):
            for copy in copies(*which):
                copy.wait_send()

        def add(block, p, which, *slots):
            combine(block, p, [[array[0](array[which], slot, p) for array in arrays] for slot in slots])

        def spread(zz):
            def across(i):
                yy = jnp.where(i == 0, 1 - y, y)
                compute_other(at(zz, yy, 1 - core))
                begin(0, None, zz, yy)

            def here(i):
                yy = jnp.where(i == 0, 1 - y, y)
                block = at(zz, yy, core)
                compute(block)

                received(0, None, zz, yy)
                combine(block, None, [[array[2].at[2 * zz + yy] for array in arrays]])
                pl.when(i == 0)(lambda: loop(count, lambda p: begin(1, p, zz)))

            loop(2, across)
            loop(2, here)

        def along(zz):
            block = at(zz, y, core)

            def one(p):
                received(1, p, zz)
                add(block, p, 3, zz)
                pl.when(zz != z)(lambda: begin(2, p, zz))

            loop(count, one)

        def step(i):
            pl.when(i < depth)(lambda: spread(farthest(i)))
            pl.when(i > 0)(lambda: along(farthest(i - 1)))

        loop(depth + 1, step)

        def last(p):
            others(lambda zz: received(3, p, zz))
            add(me, p, 4, *[lax.rem(z + k, depth) for k in range(1, depth)])
            finish(p)

        loop(count, last)

        def drain():
            def one(zz):
                sent(0, None, zz, 0)
                sent(0, None, zz, 1)
                sent(1, None, zz)
                pl.when(zz != z)(lambda: sent(2, None, zz))

            loop(depth, one)

        drains.append(drain)

    def project(gathered, weight, load):
        acc[...] = jnp.zeros_like(acc)

        def term(block):
            depth_rows = pl.ds(pl.multiple_of(block * width, width), width)
            acc[...] += jnp.dot(
                gathered.buffer[block], weight[depth_rows, :], preferred_element_type=F32
            )

        gathered.run(load.wait, term, term, depth)
        mean = lay_column(jnp.sum(gathered.extra[...], axis=0)) * (1.0 / features)
        return acc[...] * lax.rsqrt(mean + EPSILON)

    gather_first = Gather(first, pieces, first_squares)
    gather_queries = Gather(queries_all, heads)
    gather_second = Gather(second, pieces, second_squares)

    loop(pieces, gather_first.begin)
    gather_first.begin(None)
    factor = head_dim**-0.5 * math.log2(math.e)
    first_block = me * (tokens // BLK)
    chunk = min(2 * rows, heads * rows)
    lanes = lax.broadcasted_iota(jnp.int32, (rows, BLK), 1)
    limit_rows = lay_column(limit_ref[...])
    for start in range(0, chunk, rows):
        bias[start : start + rows, :] = jnp.where(limit_rows >= first_block + lanes, 0.0, -1e30).astype(BF16)
    lanes = lax.broadcasted_iota(jnp.int32, (BLK, BLK), 1)
    for j in range(tokens // BLK):
        marks[j * BLK : (j + 1) * BLK, :] = jnp.where(lanes == j, 1.0, 0.0).astype(BF16)

    query = project(gather_first, qw, loads[0])
    for head in range(heads):
        one = query[:, head * head_dim : (head + 1) * head_dim]
        mean = jnp.mean(one * one, axis=1, keepdims=True)
        queries_all[me, head * rows : (head + 1) * rows, :] = (
            one * lax.rsqrt(mean + EPSILON) * (q_gain_ref[...].astype(F32) * factor)
        ).astype(BF16)
        gather_queries.begin(head)

    def attend(block):
        group = (block * heads) // group_size
        columns = pl.ds(pl.multiple_of(group * head_dim, head_dim), head_dim)
        for start in range(0, heads * rows, chunk):
            query_rows = jnp.concatenate([queries_all[block, start : start + chunk, :], bias[...]], axis=1)
            marked = jnp.concatenate([keys[:, columns], marks[...]], axis=1)
            scores = lax.dot_general(
                query_rows, marked, (((1,), (1,)), ((), ())), preferred_element_type=F32
            )
            tiles = [scores[:, j * BLK : (j + 1) * BLK] for j in range(tokens // BLK)]
            top = functools.reduce(jnp.maximum, tiles)
            top = jnp.max(top, axis=1, keepdims=True)
            tiles = [jnp.exp2(tile - top) for tile in tiles]
            total = jnp.sum(functools.reduce(jnp.add, tiles), axis=1, keepdims=True)
            weights = jnp.concatenate([tile.astype(BF16) for tile in tiles], axis=1)
            summed = jnp.dot(weights, values[:, columns], preferred_element_type=F32)
            sums[block, start : start + chunk, :] = summed.astype(BF16)
            for inner in range(0, chunk, rows):
                head = (start + inner) // rows
                stats[block, head, 0:1, :] = lay_row(top[inner : inner + rows, :])
                stats[block, head, 1:2, :] = lay_row(total[inner : inner + rows, :])

    def span(head):
        start = head * rows
        return pl.ds(start if isinstance(head, int) else pl.multiple_of(start, rows), rows)

    def merge(block, head, arrived):
        if head is None:
            for one in range(heads):
                merge(block, one, [[span_sums.at[span(one)], span_stats.at[one]] for span_sums, span_stats in arrived])
            return
        marks_all = [stats[block, head]] + [pair[1][...] for pair in arrived]
        sums_all = [sums[block, span(head), :]] + [pair[0][...] for pair in arrived]
        top = functools.reduce(jnp.maximum, [mark[:1] for mark in marks_all])
        decays = [jnp.exp2(mark[:1] - top) for mark in marks_all]
        stats[block, head, 0:1, :] = top
        stats[block, head, 1:2, :] = sum(mark[1:2] * decay for mark, decay in zip(marks_all, decays))
        sums[block, span(head), :] = sum(
            part.astype(F32) * lay_column(decay) for part, decay in zip(sums_all, decays)
        ).astype(BF16)

    def caches_ready():
        loads[1].wait()
        loads[2].wait()

    gather_queries.run(caches_ready, attend, attend, 1)

    def attend_late(block):
        @pl.when(block // 4 != z)
        def _():
            gather_queries.arrive_all(block)
            attend(block)

    def close(head):
        total = lay_column(stats[me, head, 1:2, :])
        attended[:, pl.ds(pl.multiple_of(head * head_dim, head_dim), head_dim)] = (
            sums[me, span(head), :].astype(F32) / total
        ).astype(BF16)

    def head_view(ref, block, p):
        return ref.at[block, span(p)]

    def stat_view(ref, block, p):
        return ref.at[block, p]

    reduce(
        [
            (head_view, sums, sums_core, sums_y, sums_z),
            (stat_view, stats, stats_core, stats_y, stats_z),
        ],
        heads,
        attend_late,
        lambda block: None,
        merge,
        close,
    )
    loads[3].wait()

    piece = rows // pieces

    def piece_rows(p):
        return pl.ds(pl.multiple_of(p * piece, piece), piece)

    def row_view(ref, block, p):
        return ref.at[block, piece_rows(p)]

    def mix(block):
        columns = pl.ds(pl.multiple_of(block * width, width), width)
        mixed[block] = jnp.dot(
            attended[...], ow[:, columns], preferred_element_type=F32
        ).astype(BF16)

    def total_of(block, p, arrived):
        span_rows = slice(None) if p is None else piece_rows(p)
        mixed[block, span_rows, :] = sum(
            (one[0][...].astype(F32) for one in arrived), mixed[block, span_rows, :].astype(F32)
        ).astype(BF16)

    def renew(p):
        span_rows = piece_rows(p)
        fresh = (hidden_in[span_rows, :].astype(F32) + mixed[me, span_rows, :].astype(F32)).astype(BF16)
        hidden_out[span_rows, :] = fresh
        fresh = fresh.astype(F32)
        second[me, span_rows, :] = (fresh * wide(next_gain_ref)).astype(BF16)
        squares[span_rows, :] = lane_sums(fresh)
        gather_second.begin(p)

    reduce(
        [(row_view, mixed, mixed_core, mixed_y, mixed_z)], pieces, mix, mix, total_of, renew
    )
    second_squares[me] = lay_row(jnp.sum(squares[...], axis=1, keepdims=True))
    gather_second.begin(None)
    next_out[...] = project(gather_second, nw, loads[4]).astype(BF16)
    for drain in drains:
        drain()


def on_device(
    hidden,
    attn_gain,
    q_weight,
    q_gain,
    key_cache,
    value_cache,
    block_limit,
    out_weight,
    next_gain,
    next_weight,
):
    n = lax.axis_size("ctx")
    depth = n // 4
    rows, width = hidden.shape
    head_dim = q_gain.shape[0]
    heads = width // head_dim
    group_size = heads * n // (key_cache.shape[1] // head_dim)
    tall, pieces = heads * rows, 4

    def slots(count):
        return [
            pltpu.VMEM((count, tall, head_dim), BF16),
            pltpu.VMEM((count, heads, 2, rows), F32),
            pltpu.VMEM((count, rows, width), BF16),
        ]

    semaphores = 2 * n * (pieces + 1) + n * heads + 20 * depth + 2 * depth * (2 * heads + pieces + 9)
    vmem, hbm = pl.BlockSpec(memory_space=pltpu.VMEM), pl.BlockSpec(memory_space=pl.ANY)
    outs = pl.pallas_call(
        functools.partial(kernel, n, group_size, pieces),
        out_shape=[jax.ShapeDtypeStruct((rows, width), BF16)] * 2,
        in_specs=[vmem] * 5 + [hbm] * 5,
        out_specs=[vmem] * 2,
        scratch_shapes=[
            pltpu.VMEM(q_weight.shape, BF16),
            pltpu.VMEM(key_cache.shape, BF16),
            pltpu.VMEM(value_cache.shape, BF16),
            pltpu.VMEM(out_weight.shape, BF16),
            pltpu.VMEM(next_weight.shape, BF16),
            pltpu.VMEM((n, rows, width), BF16),
            pltpu.VMEM((n, 1, rows), F32),
            pltpu.VMEM((n, tall, head_dim), BF16),
            pltpu.VMEM((n, rows, width), BF16),
            pltpu.VMEM((n, 1, rows), F32),
            *slots(n),
            *slots(2 * depth),
            *slots(depth),
            *slots(depth),
            pltpu.VMEM((rows, width), F32),
            pltpu.VMEM((rows, BLK), F32),
            pltpu.VMEM((min(2 * rows, tall), BLK), BF16),
            pltpu.VMEM((key_cache.shape[0], BLK), BF16),
            pltpu.VMEM((rows, width), BF16),
            pltpu.SemaphoreType.DMA((semaphores,)),
            pltpu.SemaphoreType.DMA((5,)),
        ],
        compiler_params=pltpu.CompilerParams(
            collective_id=0, has_side_effects=True, vmem_limit_bytes=67043328
        ),
    )(
        hidden,
        attn_gain.reshape(-1, BLK),
        next_gain.reshape(-1, BLK),
        q_gain[None],
        block_limit[None],
        q_weight,
        key_cache,
        value_cache,
        out_weight,
        next_weight,
    )
    return pl.pallas_call(
        hand_over,
        out_shape=[jax.ShapeDtypeStruct((rows, width), BF16)] * 2,
        in_specs=[vmem] * 2,
        out_specs=[vmem] * 2,
    )(*outs)


def hand_over(hidden_in, next_in, hidden_out, next_out):
    hidden_out[...] = hidden_in[...]
    next_out[...] = next_in[...]


def solution(mesh):
    in_specs = (
        P("groups", "ctx"),
        P("ctx"),
        P(None, "ctx"),
        P(),
        P(("groups", "ctx"), None),
        P(("groups", "ctx"), None),
        P("groups"),
        P("ctx", None),
        P("ctx"),
        P(None, "ctx"),
    )
    out_specs = (P("groups", "ctx"), P("groups", "ctx"))

    def step(*args):
        return tuple(on_device(*args))

    return jax.shard_map(step, mesh=mesh, in_specs=in_specs, out_specs=out_specs, check_vma=False)
```

```python
import functools
import math

import jax
import jax.numpy as jnp
from jax import lax
from jax.experimental import pallas as pl
from jax.experimental.pallas import tpu as pltpu
from jax.sharding import PartitionSpec as P

BLK = 128
EPSILON = 1e-05
MESH = pl.DeviceIdType.MESH
BF16, F32 = jnp.bfloat16, jnp.float32


def loop(count, body):
    def step(i, carry):
        body(i)
        return carry

    lax.fori_loop(0, count, step, 0)


def kernel(
    n,
    group_size,
    pieces,
    hidden_in,
    attn_gain_ref,
    next_gain_ref,
    q_gain_ref,
    limit_ref,
    qw_hbm,
    key_hbm,
    value_hbm,
    ow_hbm,
    nw_hbm,
    hidden_out,
    next_out,
    qw,
    keys,
    values,
    ow,
    nw,
    first,
    first_squares,
    queries_all,
    second,
    second_squares,
    sums,
    stats,
    mixed,
    sums_core,
    stats_core,
    mixed_core,
    sums_y,
    stats_y,
    mixed_y,
    sums_z,
    stats_z,
    mixed_z,
    acc,
    squares,
    bias,
    marks,
    attended,
    sems,
    local_sems,
):
    depth = n // 4
    me = lax.axis_index("ctx")
    core, y, z = lax.rem(me, 2), lax.rem(me // 2, 2), me // 4
    rows, width = hidden_out.shape
    features = n * width
    head_dim = q_gain_ref.shape[1]
    heads = width // head_dim
    tokens = keys.shape[0]

    def at(zz, yy, cc):
        return zz * 4 + yy * 2 + cc

    other_core, other_y = at(z, y, 1 - core), at(z, 1 - y, core)

    def others(action):
        def one(zz):
            pl.when(zz != z)(lambda: action(zz))

        loop(depth, one)

    loads = [
        pltpu.make_async_copy(src, dst, local_sems.at[i])
        for i, (src, dst) in enumerate(
            [(qw_hbm, qw), (key_hbm, keys), (value_hbm, values), (ow_hbm, ow), (nw_hbm, nw)]
        )
    ]
    for load in loads:
        load.start()

    barrier = pltpu.get_barrier_semaphore()

    def greet(device):
        pl.semaphore_signal(barrier, inc=1, device_id={"ctx": device}, device_id_type=MESH)

    greet(other_core)
    greet(other_y)
    others(lambda zz: greet(at(zz, y, core)))

    def near(action):
        def one(zz):
            pl.when((zz != z) & (jnp.abs(zz - z) <= 2))(lambda: action(zz))

        loop(depth, one)

    def wide(gain):
        lines = gain[...].astype(F32)
        return jnp.concatenate([lines[i : i + 1, :] for i in range(lines.shape[0])], axis=1)

    def lay_row(column):
        return jnp.broadcast_to(column, (rows, rows)).T[:1, :]

    def lay_column(row):
        return jnp.broadcast_to(row, (rows, rows)).T[:, :1]

    def lane_sums(part):
        squared = part * part
        total = squared[:, :BLK]
        for start in range(BLK, width, BLK):
            total += squared[:, start : start + BLK]
        return total

    own = hidden_in[...].astype(F32)
    first[me] = (own * wide(attn_gain_ref)).astype(BF16)

    pl.semaphore_wait(barrier, depth + 1)

    before, after = z, depth - 1 - z
    lone, paired = jnp.abs(after - before), jnp.minimum(after, before)

    def farthest(i):
        j = jnp.maximum(i - lone, 0)
        distance = paired - lax.div(j, 2)
        near = z + jnp.where(lax.rem(j, 2) == 0, distance, -distance)
        return jnp.where(i < lone, jnp.where(after > before, depth - 1 - i, i), near)

    def remote(src, dst, send, recv, device):
        return pltpu.make_async_remote_copy(
            src_ref=src,
            dst_ref=dst,
            send_sem=sems.at[send],
            recv_sem=sems.at[recv],
            device_id={"ctx": device},
            device_id_type=MESH,
        )

    used = [0]
    drains = []

    def take(count):
        used[0] += count
        return used[0] - count

    class Gather:
        def __init__(self, buffer, count, extra=None):
            self.buffer, self.count, self.extra = buffer, count, extra
            self.size = buffer.shape[1] // count
            self.recv, self.send = take(n * count), take(5 * depth)
            if extra is not None:
                self.extra_recv, self.extra_send = take(n), take(5 * depth)
            drains.append(self.drain)

        def copy(self, block, p, device, sem):
            view = self.buffer.at[block, pl.ds(pl.multiple_of(p * self.size, self.size), self.size)]
            return remote(view, view, self.send + sem, self.recv + block * self.count + p, device)

        def extra_copy(self, block, device, sem):
            view = self.extra.at[block]
            return remote(view, view, self.extra_send + sem, self.extra_recv + block, device)

        def whole(self, block, device, sem):
            view = self.buffer.at[block]
            return remote(view, view, self.send + sem, self.recv, device)

        def to_z(self, zz):
            return me, at(zz, y, core), zz

        def outward(self, zz):
            beyond = jnp.where(zz < z, z + 1, z - 1)
            return at(zz, y, core), at(beyond, y, core), 4 * depth + zz

        def passes_on(self, zz):
            return (jnp.abs(zz - z) >= 2) & jnp.where(zz < z, z + 1 < depth, z > 0)

        def to_y(self, zz):
            return at(zz, y, core), other_y, depth + zz

        def to_core(self, zz, yy):
            return at(zz, yy, core), other_core, 2 * depth + 2 * zz + yy

        def start(self, route, p):
            block, device, sem = route
            if p is None:
                self.extra_copy(block, device, sem).start()
            else:
                self.copy(block, p, device, sem).start()

        def arrive(self, block, p):
            if p is None:
                self.extra_copy(block, other_core, 0).wait_recv()
            else:
                self.copy(block, p, other_core, 0).wait_recv()

        def arrive_all(self, block):
            loop(self.count, lambda p: self.arrive(block, p))
            if self.extra is not None:
                self.arrive(block, None)

        def begin(self, p):
            self.start(self.to_y(z), p)
            near(lambda zz: self.start(self.to_z(zz), p))
            self.start(self.to_core(z, y), p)

        def column(self, distance, sign, p):
            zz = z + sign * distance

            @pl.when((zz >= 0) & (zz < depth))
            def _():
                self.arrive(at(zz, y, core), p)
                pl.when(self.passes_on(zz))(lambda: self.start(self.outward(zz), p))
                self.start(self.to_y(zz), p)
                self.start(self.to_core(zz, y), p)

        def beside(self, distance, sign, p):
            zz = z + sign * distance
            fresh = (distance > 0) if sign > 0 else (distance >= 0)

            @pl.when((zz >= 0) & (zz < depth) & fresh)
            def _():
                self.arrive(at(zz, 1 - y, core), p)
                self.start(self.to_core(zz, 1 - y), p)

        def run(self, ready, consume, consume_late, reach):
            def pair(distance, yy, cc, use):
                def one(i):
                    zz = z + jnp.where(i == 0, -distance, distance)
                    fresh = (distance > 0) | ((distance == 0) & (i == 0))

                    @pl.when(fresh & (zz >= 0) & (zz < depth))
                    def _():
                        use(at(zz, yy, cc))

                loop(2, one)

            def late(block):
                self.arrive_all(block)
                consume_late(block)

            def relay(step, p):
                self.column(step, -1, p)
                self.column(step, 1, p)
                self.beside(step - 1, -1, p)
                self.beside(step - 1, 1, p)

            def turn(i):
                step = i + 1

                def inner(p):
                    pl.when(step <= depth)(lambda: relay(step, p))
                    pl.when((step == 1) & (p == 0))(ready)
                    for k in range(4):
                        slot = (k * self.count) // 4

                        @pl.when(p == slot)
                        def _():
                            if k == 0:
                                pair(step - 1, y, core, consume)
                            elif k == 1:
                                pair(step - 2, 1 - y, core, consume)
                            elif k == 2:
                                pl.when(step - 2 < reach)(lambda: pair(step - 2, y, 1 - core, late))
                            else:
                                pl.when(step - 3 < reach)(lambda: pair(step - 3, 1 - y, 1 - core, late))

                loop(self.count, inner)
                if self.extra is not None:
                    pl.when(step <= depth)(lambda: relay(step, None))

            loop(max(depth + 1, reach + 2), turn)

        def drain(self):
            kinds = [self.whole]
            if self.extra is not None:
                kinds.append(self.extra_copy)

            def one(zz):
                for kind in kinds:
                    pl.when((zz != z) & (jnp.abs(zz - z) <= 2))(lambda: kind(*self.to_z(zz)).wait_send())
                    pl.when(self.passes_on(zz))(lambda: kind(*self.outward(zz)).wait_send())
                    kind(*self.to_y(zz)).wait_send()
                    kind(*self.to_core(zz, 0)).wait_send()
                    kind(*self.to_core(zz, 1)).wait_send()

            loop(depth, one)

    def reduce(arrays, count, compute_other, compute, combine, finish):
        starts = [(take(4 * depth), take(2 * depth + 2 * depth * count)) for _ in arrays]

        def copies(kind, p, zz, yy=0):
            made = []
            for (send, recv), (view, part, from_core, from_y, from_z) in zip(starts, arrays):
                sender = slot = zz
                if kind == 0:
                    sender = slot = 2 * zz + yy
                    where, block, dst, device = 0, at(zz, yy, 1 - core), from_core, other_core
                elif kind == 1:
                    where, block, dst, device = 2 * depth, at(zz, 1 - y, core), from_y, other_y
                else:
                    where, block, dst, device = 3 * depth, at(zz, y, core), from_z, at(zz, y, core)
                    slot = z if kind == 2 else zz
                if p is None:
                    src, dst, arrival = part.at[block], dst.at[slot], slot if kind == 0 else 0
                else:
                    src, dst = view(part, block, p), view(dst, slot, p)
                    arrival = 2 * depth + (where - 2 * depth + slot) * count + p
                made.append(remote(src, dst, send + where + sender, recv + arrival, device))
            return made

        def begin(*which):
            for copy in copies(*which):
                copy.start()

        def received(*which):
            for copy in copies(*which):
                copy.wait_recv()

        def sent(*which):
            for copy in copies(*which):
                copy.wait_send()

        def add(block, p, which, *slots):
            combine(block, p, [[array[0](array[which], slot, p) for array in arrays] for slot in slots])

        def spread(zz):
            def across(i):
                yy = jnp.where(i == 0, 1 - y, y)
                compute_other(at(zz, yy, 1 - core))
                begin(0, None, zz, yy)

            def here(i):
                yy = jnp.where(i == 0, 1 - y, y)
                block = at(zz, yy, core)
                compute(block)

                received(0, None, zz, yy)
                combine(block, None, [[array[2].at[2 * zz + yy] for array in arrays]])
                pl.when(i == 0)(lambda: loop(count, lambda p: begin(1, p, zz)))

            loop(2, across)
            loop(2, here)

        def along(zz):
            block = at(zz, y, core)

            def one(p):
                received(1, p, zz)
                add(block, p, 3, zz)
                pl.when(zz != z)(lambda: begin(2, p, zz))

            loop(count, one)

        def step(i):
            pl.when(i < depth)(lambda: spread(farthest(i)))
            pl.when(i > 0)(lambda: along(farthest(i - 1)))

        loop(depth + 1, step)

        def last(p):
            others(lambda zz: received(3, p, zz))
            add(me, p, 4, *[lax.rem(z + k, depth) for k in range(1, depth)])
            finish(p)

        loop(count, last)

        def drain():
            def one(zz):
                sent(0, None, zz, 0)
                sent(0, None, zz, 1)
                sent(1, None, zz)
                pl.when(zz != z)(lambda: sent(2, None, zz))

            loop(depth, one)

        drains.append(drain)

    def project(gathered, weight, load):
        acc[...] = jnp.zeros_like(acc)

        def term(block):
            depth_rows = pl.ds(pl.multiple_of(block * width, width), width)
            acc[...] += jnp.dot(
                gathered.buffer[block], weight[depth_rows, :], preferred_element_type=F32
            )

        gathered.run(load.wait, term, term, depth)
        mean = lay_column(jnp.sum(gathered.extra[...], axis=0)) * (1.0 / features)
        return acc[...] * lax.rsqrt(mean + EPSILON)

    gather_first = Gather(first, pieces, first_squares)
    gather_queries = Gather(queries_all, heads)
    gather_second = Gather(second, pieces, second_squares)

    loop(pieces, gather_first.begin)
    first_squares[me] = lay_row(jnp.sum(lane_sums(own), axis=1, keepdims=True))
    gather_first.begin(None)
    factor = head_dim**-0.5 * math.log2(math.e)
    first_block = me * (tokens // BLK)
    chunk = min(2 * rows, heads * rows)
    lanes = lax.broadcasted_iota(jnp.int32, (rows, BLK), 1)
    limit_rows = lay_column(limit_ref[...])
    for start in range(0, chunk, rows):
        bias[start : start + rows, :] = jnp.where(limit_rows >= first_block + lanes, 0.0, -1e30).astype(BF16)
    lanes = lax.broadcasted_iota(jnp.int32, (BLK, BLK), 1)
    for j in range(tokens // BLK):
        marks[j * BLK : (j + 1) * BLK, :] = jnp.where(lanes == j, 1.0, 0.0).astype(BF16)

    query = project(gather_first, qw, loads[0])
    for head in range(heads):
        one = query[:, head * head_dim : (head + 1) * head_dim]
        mean = jnp.mean(one * one, axis=1, keepdims=True)
        queries_all[me, head * rows : (head + 1) * rows, :] = (
            one * lax.rsqrt(mean + EPSILON) * (q_gain_ref[...].astype(F32) * factor)
        ).astype(BF16)
        gather_queries.begin(head)

    def attend(block):
        group = (block * heads) // group_size
        columns = pl.ds(pl.multiple_of(group * head_dim, head_dim), head_dim)
        for start in range(0, heads * rows, chunk):
            query_rows = jnp.concatenate([queries_all[block, start : start + chunk, :], bias[...]], axis=1)
            marked = jnp.concatenate([keys[:, columns], marks[...]], axis=1)
            scores = lax.dot_general(
                query_rows, marked, (((1,), (1,)), ((), ())), preferred_element_type=F32
            )
            tiles = [scores[:, j * BLK : (j + 1) * BLK] for j in range(tokens // BLK)]
            top = functools.reduce(jnp.maximum, tiles)
            top = jnp.max(top, axis=1, keepdims=True)
            tiles = [jnp.exp2(tile - top) for tile in tiles]
            total = jnp.sum(functools.reduce(jnp.add, tiles), axis=1, keepdims=True)
            weights = jnp.concatenate([tile.astype(BF16) for tile in tiles], axis=1)
            summed = jnp.dot(weights, values[:, columns], preferred_element_type=F32)
            sums[block, start : start + chunk, :] = summed.astype(BF16)
            for inner in range(0, chunk, rows):
                head = (start + inner) // rows
                stats[block, head, 0:1, :] = lay_row(top[inner : inner + rows, :])
                stats[block, head, 1:2, :] = lay_row(total[inner : inner + rows, :])

    def span(head):
        start = head * rows
        return pl.ds(start if isinstance(head, int) else pl.multiple_of(start, rows), rows)

    def merge(block, head, arrived):
        if head is None:
            for one in range(heads):
                merge(block, one, [[span_sums.at[span(one)], span_stats.at[one]] for span_sums, span_stats in arrived])
            return
        marks_all = [stats[block, head]] + [pair[1][...] for pair in arrived]
        sums_all = [sums[block, span(head), :]] + [pair[0][...] for pair in arrived]
        top = functools.reduce(jnp.maximum, [mark[:1] for mark in marks_all])
        decays = [jnp.exp2(mark[:1] - top) for mark in marks_all]
        stats[block, head, 0:1, :] = top
        stats[block, head, 1:2, :] = sum(mark[1:2] * decay for mark, decay in zip(marks_all, decays))
        sums[block, span(head), :] = sum(
            part.astype(F32) * lay_column(decay) for part, decay in zip(sums_all, decays)
        ).astype(BF16)

    def caches_ready():
        loads[1].wait()
        loads[2].wait()

    gather_queries.run(caches_ready, attend, attend, 1)

    def attend_late(block):
        @pl.when(block // 4 != z)
        def _():
            gather_queries.arrive_all(block)
            attend(block)

    def close(head):
        total = lay_column(stats[me, head, 1:2, :])
        attended[:, pl.ds(pl.multiple_of(head * head_dim, head_dim), head_dim)] = (
            sums[me, span(head), :].astype(F32) / total
        ).astype(BF16)

    def head_view(ref, block, p):
        return ref.at[block, span(p)]

    def stat_view(ref, block, p):
        return ref.at[block, p]

    reduce(
        [
            (head_view, sums, sums_core, sums_y, sums_z),
            (stat_view, stats, stats_core, stats_y, stats_z),
        ],
        heads,
        attend_late,
        lambda block: None,
        merge,
        close,
    )
    loads[3].wait()

    piece = rows // pieces

    def piece_rows(p):
        return pl.ds(pl.multiple_of(p * piece, piece), piece)

    def row_view(ref, block, p):
        return ref.at[block, piece_rows(p)]

    def mix(block):
        columns = pl.ds(pl.multiple_of(block * width, width), width)
        mixed[block] = jnp.dot(
            attended[...], ow[:, columns], preferred_element_type=F32
        ).astype(BF16)

    def total_of(block, p, arrived):
        span_rows = slice(None) if p is None else piece_rows(p)
        mixed[block, span_rows, :] = sum(
            (one[0][...].astype(F32) for one in arrived), mixed[block, span_rows, :].astype(F32)
        ).astype(BF16)

    def renew(p):
        span_rows = piece_rows(p)
        fresh = (hidden_in[span_rows, :].astype(F32) + mixed[me, span_rows, :].astype(F32)).astype(BF16)
        hidden_out[span_rows, :] = fresh
        fresh = fresh.astype(F32)
        second[me, span_rows, :] = (fresh * wide(next_gain_ref)).astype(BF16)
        squares[span_rows, :] = lane_sums(fresh)
        gather_second.begin(p)

    reduce(
        [(row_view, mixed, mixed_core, mixed_y, mixed_z)], pieces, mix, mix, total_of, renew
    )
    second_squares[me] = lay_row(jnp.sum(squares[...], axis=1, keepdims=True))
    gather_second.begin(None)
    next_out[...] = project(gather_second, nw, loads[4]).astype(BF16)
    for drain in drains:
        drain()


def on_device(
    hidden,
    attn_gain,
    q_weight,
    q_gain,
    key_cache,
    value_cache,
    block_limit,
    out_weight,
    next_gain,
    next_weight,
):
    n = lax.axis_size("ctx")
    depth = n // 4
    rows, width = hidden.shape
    head_dim = q_gain.shape[0]
    heads = width // head_dim
    group_size = heads * n // (key_cache.shape[1] // head_dim)
    tall, pieces = heads * rows, 4

    def slots(count):
        return [
            pltpu.VMEM((count, tall, head_dim), BF16),
            pltpu.VMEM((count, heads, 2, rows), F32),
            pltpu.VMEM((count, rows, width), BF16),
        ]

    semaphores = 2 * n * (pieces + 1) + n * heads + 25 * depth + 2 * depth * (2 * heads + pieces + 9)
    vmem, hbm = pl.BlockSpec(memory_space=pltpu.VMEM), pl.BlockSpec(memory_space=pl.ANY)
    outs = pl.pallas_call(
        functools.partial(kernel, n, group_size, pieces),
        out_shape=[jax.ShapeDtypeStruct((rows, width), BF16)] * 2,
        in_specs=[vmem] * 5 + [hbm] * 5,
        out_specs=[vmem] * 2,
        scratch_shapes=[
            pltpu.VMEM(q_weight.shape, BF16),
            pltpu.VMEM(key_cache.shape, BF16),
            pltpu.VMEM(value_cache.shape, BF16),
            pltpu.VMEM(out_weight.shape, BF16),
            pltpu.VMEM(next_weight.shape, BF16),
            pltpu.VMEM((n, rows, width), BF16),
            pltpu.VMEM((n, 1, rows), F32),
            pltpu.VMEM((n, tall, head_dim), BF16),
            pltpu.VMEM((n, rows, width), BF16),
            pltpu.VMEM((n, 1, rows), F32),
            *slots(n),
            *slots(2 * depth),
            *slots(depth),
            *slots(depth),
            pltpu.VMEM((rows, width), F32),
            pltpu.VMEM((rows, BLK), F32),
            pltpu.VMEM((min(2 * rows, tall), BLK), BF16),
            pltpu.VMEM((key_cache.shape[0], BLK), BF16),
            pltpu.VMEM((rows, width), BF16),
            pltpu.SemaphoreType.DMA((semaphores,)),
            pltpu.SemaphoreType.DMA((5,)),
        ],
        compiler_params=pltpu.CompilerParams(
            collective_id=0, has_side_effects=True, vmem_limit_bytes=67043328
        ),
    )(
        hidden,
        attn_gain.reshape(-1, BLK),
        next_gain.reshape(-1, BLK),
        q_gain[None],
        block_limit[None],
        q_weight,
        key_cache,
        value_cache,
        out_weight,
        next_weight,
    )
    return pl.pallas_call(
        hand_over,
        out_shape=[jax.ShapeDtypeStruct((rows, width), BF16)] * 2,
        in_specs=[vmem] * 2,
        out_specs=[vmem] * 2,
    )(*outs)


def hand_over(hidden_in, next_in, hidden_out, next_out):
    hidden_out[...] = hidden_in[...]
    next_out[...] = next_in[...]


def solution(mesh):
    in_specs = (
        P("groups", "ctx"),
        P("ctx"),
        P(None, "ctx"),
        P(),
        P(("groups", "ctx"), None),
        P(("groups", "ctx"), None),
        P("groups"),
        P("ctx", None),
        P("ctx"),
        P(None, "ctx"),
    )
    out_specs = (P("groups", "ctx"), P("groups", "ctx"))

    def step(*args):
        return tuple(on_device(*args))

    return jax.shard_map(step, mesh=mesh, in_specs=in_specs, out_specs=out_specs, check_vma=False)
```
